32 devices in a mesh: grp: 4 (over z), band: 8 (over y, x, core).
Axes of the slice: x: 2, y: 2, z: 4, core: 2. Of those that a mesh axis runs over, the one named last changes fastest.
Arguments:
- latent: bfloat16 [16384, 512], P(('grp', 'band')), may hold values from -6 to 6
- obs_feat: bfloat16 [4096, 512], P(('grp', 'band')), may hold values from -6 to 6
- obs_bias: bfloat16 [4096], P(('grp', 'band')), may hold values from -240 to 240
- obs_route: int32 [512, 1], P(('grp', 'band')), may hold values from 0 to 7; in each aligned block of 16 rows (0 to 15, 16 to 31, ...) at most 2 rows name the same one
- obs_tile_mask: int32 [512, 8], P(('grp', 'band')), may hold values 0 or 1
- w_query: bfloat16 [512, 512], replicated, may hold values from -0.25 to 0.25
- w_key: bfloat16 [512, 512], replicated, may hold values from -0.25 to 0.25
- w_value: bfloat16 [512, 512], replicated, may hold values from -0.25 to 0.25
- w_out: bfloat16 [512, 512], replicated, may hold values from -0.25 to 0.25
- grad_out: bfloat16 [16384, 512], P(('grp', 'band')), may hold values from -6 to 6
Outputs:
- attended: bfloat16 [16384, 512], P(('grp', 'band'))
- grad_latent: bfloat16 [16384, 512], P(('grp', 'band'))
- grad_obs: bfloat16 [4096, 512], P(('grp', 'band'))
- grad_weights: float32 [2048, 512], P('band')
The draws below stay inside these ranges and needn't reach their ends.
Inputs may be any that keep to these rules, and one draw needn't show every extreme that they name: `obs_route`: among the 16 blocks of one device no band is named more than 2 times, a bound that some block reaches by some device in every draw.
All inputs are finite; a program needn't handle non-finite values. No bound on the sum of `obs_tile_mask` on one device may be relied on, other than what follows from the above.
Results may differ from the reference program's by a relative error of at most 0.023.
Values may be sent and summed in bfloat16 or wider, within the bound.
A program may use at most 64 MiB of HBM per device.

```python
import math
import jax
import jax.numpy as jnp
import numpy as np
from jax import lax

D = 512
HEADS = 16
LAT_DEV = 512
QTILE = 64
OB = 8
SRC_BLK = 16
CAP = 2
NQT = 8
LATENT = 16384
ALLBLK = 512
ALLOBS = 4096
N_GRP = 4
N_BAND = 8


def draw_obs_bias(key, part):
    base = jax.random.normal(key, (ALLOBS,), jnp.float32)
    return base.astype(jnp.bfloat16)


def place_ends(array, rng, smallest, largest):
    place = [jax.random.randint(jax.random.fold_in(rng, axis), (), 0, length) for axis, length in enumerate(array.shape)]
    widest = array.shape.index(max(array.shape))
    neighbour = place[:widest] + [(place[widest] + 1) % array.shape[widest]] + place[widest + 1:]
    return array.at[tuple(place)].set(smallest).at[tuple(neighbour)].set(largest)


def block_scale(stream_key, shape, shards, least, top_value):
    loudness = 1.0
    for axis_at, blocks in shards:
        draws = jax.random.uniform(jax.random.fold_in(jax.random.fold_in(stream_key, 6), axis_at), (blocks,), jnp.float32, least / len(shards), top_value / len(shards))
        loudness = loudness * jnp.repeat(jnp.exp(draws), shape[axis_at] // blocks).reshape((-1,) + (1,) * (len(shape) - 1 - axis_at))
    return loudness


def assign_block(own_key, own, number, rows, count, top, reach, slope):
    ranking = jax.random.permutation(own_key, count)
    crowded, common = load_shares(count, rows * top, reach, slope, True), load_shares(count, rows * top, reach, slope, False)
    places = jnp.arange(count)

    def named(tallies, turn):
        used = int((tallies > 0).sum())
        fixed = max(1, used // 4)
        moved = fixed + (places - fixed + turn * (used - fixed)) % max(1, count - fixed)
        return jnp.zeros((count,), jnp.int32).at[ranking[jnp.where(places < fixed, places, moved)]].set(jnp.asarray(tallies, jnp.int32))

    tallies = jnp.where(number % 4 == 0, named(crowded, number // 4), named(common, number - number // 4 - 1))
    mixed = jax.random.permutation(jax.random.fold_in(own, 3), count)
    source_of, taker = mixed[0:count // 2 * 2:2], mixed[1:count // 2 * 2:2]
    room = jnp.minimum(tallies[source_of] - 1, reach - tallies[taker]) // 2
    room = jnp.where((source_of == ranking[0]) | (taker == ranking[0]) | (tallies[taker] == 0), 0, jnp.maximum(room, 0))
    moved = jax.random.randint(jax.random.fold_in(own, 4), (count // 2,), 0, 1 << 20) % (room + 1)
    tallies = tallies.at[source_of].add(-moved).at[taker].add(moved)
    members = jnp.searchsorted(jnp.cumsum(tallies), jnp.arange(rows * top), side="right").astype(jnp.int32)
    listing = members.reshape(top, rows).T
    listing = listing[jax.random.permutation(jax.random.fold_in(own, 1), rows)]
    turn = jax.random.randint(jax.random.fold_in(own, 2), (rows, 1), 0, top)
    return jnp.take_along_axis(listing, (jnp.arange(top)[None, :] + turn) % top, axis=1)


def load_shares(number_of, total, bound, slope, full):
    loads = [(1 << 20) // math.isqrt(rank ** slope) + 1 for rank in range(1, number_of + 1)]
    largest = bound if full else min(bound, max(-(-total // number_of), total * loads[0] // sum(loads)))
    least = 1 if total - largest >= number_of - 1 else 0
    holding, surplus = [largest] + [least] * (number_of - 1), total - largest - least * (number_of - 1)
    while surplus > 0:
        candidates = [i for i in range(1, number_of) if holding[i] < largest] or [i for i in range(1, number_of) if holding[i] < bound]
        whole, remaining = sum([loads[i] for i in candidates]), surplus
        for i in candidates:
            extra = min(bound - holding[i], max(1, remaining * loads[i] // whole), surplus)
            holding[i] = holding[i] + extra
            surplus = surplus - extra
    return np.array(holding)


def scatter_about(rng, dims, deviation, limit, shards=(), held_as=jnp.bfloat16):
    entries = deviation * jax.random.normal(rng, dims, jnp.float32)
    if shards:
        entries = entries * block_scale(rng, dims, shards, -0.22, 0.18)
    return jnp.clip(entries, -limit, limit).astype(held_as)


def setup_inputs(seed: int = 0) -> dict:
    key_list = jax.random.split(jax.random.key(seed), 11)
    latent = scatter_about(key_list[0], (LATENT, D), 1.0, 6.0, ((0, 32),))
    obs_feat = scatter_about(key_list[1], (ALLOBS, D), 1.0, 6.0, ((0, 32),))
    obs_bias = draw_obs_bias(jax.random.fold_in(key_list[10], 71), 0)
    obs_route_keys = jax.random.split(jax.random.fold_in(key_list[3], 1), ALLBLK // SRC_BLK)
    obs_route_turns = jax.random.permutation(jax.random.fold_in(key_list[3], 3), ALLBLK // SRC_BLK)
    obs_route = jax.vmap(lambda own, number: assign_block(jax.random.fold_in(key_list[3], 2), own, number, SRC_BLK, N_BAND, 1, CAP, 2))(obs_route_keys, obs_route_turns).reshape((ALLBLK, 1))
    obs_tile_mask = place_ends((jax.random.randint(key_list[4], (ALLBLK, NQT), 0, 2) < 1).astype(jnp.int32), jax.random.fold_in(key_list[4], 1), 0, 1)
    w_query = scatter_about(key_list[5], (D, D), D ** -0.5, 0.25)
    w_key = scatter_about(key_list[6], (D, D), D ** -0.5, 0.25)
    w_value = scatter_about(key_list[7], (D, D), D ** -0.5, 0.25)
    w_out = scatter_about(key_list[8], (D, D), D ** -0.5, 0.25)
    grad_out = scatter_about(key_list[9], (LATENT, D), 1.0, 6.0, ((0, 32),))
    return {"latent": latent, "obs_feat": obs_feat, "obs_bias": obs_bias, "obs_route": obs_route, "obs_tile_mask": obs_tile_mask, "w_query": w_query, "w_key": w_key, "w_value": w_value, "w_out": w_out, "grad_out": grad_out}


def reference(latent, obs_feat, obs_bias, obs_route, obs_tile_mask, w_query, w_key, w_value, w_out, grad_out):
    devices_all = N_GRP * N_BAND
    slots = N_BAND * CAP
    key_rows = slots * OB
    head_size = D // HEADS
    scale = 1.0 / math.sqrt(head_size)
    w_pair = jnp.concatenate([w_key, w_value], axis=1)
    pair = jnp.dot(obs_feat, w_pair, preferred_element_type=jnp.float32).astype(jnp.bfloat16)
    pair_blocks = pair.reshape(devices_all * SRC_BLK, OB * 2 * D)
    bias_blocks = obs_bias.reshape(devices_all * SRC_BLK, OB)
    route = obs_route[:, 0].reshape(devices_all, SRC_BLK)
    order = jnp.arange(SRC_BLK)
    earlier = order[:, None] < order[None, :]
    rank = lax.optimization_barrier(jnp.sum(((route[:, :, None] == route[:, None, :]) & earlier[None]).astype(jnp.int32), axis=1))
    device_ids = jnp.arange(devices_all, dtype=jnp.int32)[:, None]
    dest_dev = device_ids // N_BAND * N_BAND + route
    slot_index = device_ids % N_BAND * CAP + rank
    block_ids = jnp.arange(devices_all * SRC_BLK, dtype=jnp.int32).reshape(devices_all, SRC_BLK)
    table = jnp.full((devices_all, slots), -1, jnp.int32).at[dest_dev, slot_index].set(block_ids)
    row_tile = jnp.arange(LAT_DEV) // QTILE

    def step(carry, inputs):
        grad_wq, grad_wo = carry
        rows, cotangent, blocks = inputs
        valid = blocks >= 0
        safe = jnp.maximum(blocks, 0)
        arrived = jnp.where(valid[:, None], pair_blocks[safe], jnp.zeros((), jnp.bfloat16)).reshape(key_rows, 2 * D)
        keys = arrived[:, :D].astype(jnp.float32).reshape(key_rows, HEADS, head_size)
        values = arrived[:, D:].astype(jnp.float32).reshape(key_rows, HEADS, head_size)
        key_bias = bias_blocks[safe].reshape(key_rows).astype(jnp.float32)
        tiles = obs_tile_mask[safe] * valid[:, None].astype(jnp.int32)
        slot_seen = tiles.T[row_tile]
        visible = jnp.repeat(slot_seen, OB, axis=1) > 0
        query = jnp.dot(rows, w_query, preferred_element_type=jnp.float32).astype(jnp.bfloat16)
        dattn = jnp.dot(cotangent, w_out.T, preferred_element_type=jnp.float32).astype(jnp.bfloat16)
        query_h = query.astype(jnp.float32).reshape(LAT_DEV, HEADS, head_size)
        dattn_h = dattn.astype(jnp.float32).reshape(LAT_DEV, HEADS, head_size)
        scores = jnp.einsum('qhd,khd->hqk', query_h, keys) * scale + key_bias[None, None, :]
        masked = jnp.where(visible[None], scores, -jnp.inf)
        top = jnp.maximum(lax.optimization_barrier(jnp.max(masked, axis=-1)), 0.0)
        expo = jnp.where(visible[None], jnp.exp(scores - top[..., None]), 0.0)
        total = jnp.exp(-top) + lax.optimization_barrier(jnp.sum(expo, axis=-1))
        prob = expo / total[..., None]
        prob_b = prob.astype(jnp.bfloat16).astype(jnp.float32)
        attn = jnp.einsum('hqk,khd->qhd', prob_b, values).reshape(LAT_DEV, D).astype(jnp.bfloat16)
        attended = jnp.dot(attn, w_out, preferred_element_type=jnp.float32).astype(jnp.bfloat16)
        dprob = jnp.einsum('qhd,khd->hqk', dattn_h, values)
        delta = lax.optimization_barrier(jnp.sum(prob * dprob, axis=-1))
        dscore = (prob * (dprob - delta[..., None])).astype(jnp.bfloat16).astype(jnp.float32)
        dquery = (jnp.einsum('hqk,khd->qhd', dscore, keys) * scale).reshape(LAT_DEV, D).astype(jnp.bfloat16)
        dkeys = (jnp.einsum('hqk,qhd->khd', dscore, query_h) * scale).reshape(key_rows, D).astype(jnp.bfloat16)
        dvalues = jnp.einsum('hqk,qhd->khd', prob_b, dattn_h).reshape(key_rows, D).astype(jnp.bfloat16)
        grad_lat = jnp.dot(dquery, w_query.T, preferred_element_type=jnp.float32).astype(jnp.bfloat16)
        grad_wq = grad_wq + jnp.dot(rows.T, dquery, preferred_element_type=jnp.float32)
        grad_wo = grad_wo + jnp.dot(attn.T, cotangent, preferred_element_type=jnp.float32)
        slot_grads = jnp.concatenate([dkeys, dvalues], axis=1).reshape(slots, OB * 2 * D)
        return ((grad_wq, grad_wo), (attended, grad_lat, slot_grads))
    start = (jnp.zeros((D, D), jnp.float32), jnp.zeros((D, D), jnp.float32))
    inputs = (latent.reshape(devices_all, LAT_DEV, D), grad_out.reshape(devices_all, LAT_DEV, D), table)
    (grad_wq, grad_wo), (attended, grad_lat, slot_grads) = lax.scan(step, start, inputs)
    dpair = slot_grads[dest_dev, slot_index].reshape(devices_all * SRC_BLK * OB, 2 * D)
    grad_obs = jnp.dot(dpair, w_pair.T, preferred_element_type=jnp.float32).astype(jnp.bfloat16)
    grad_pair = jnp.dot(obs_feat.T, dpair, preferred_element_type=jnp.float32)
    grads = jnp.concatenate([grad_wq, grad_pair[:, :D], grad_pair[:, D:], grad_wo], axis=0) / float(N_GRP)
    return (attended.reshape(LATENT, D), grad_lat.reshape(LATENT, D), grad_obs, grads)
```

```python
import functools
import math

import jax
import jax.numpy as jnp
from jax import lax
from jax.experimental import pallas as pl
from jax.experimental.pallas import tpu as pltpu
from jax.sharding import PartitionSpec as P

HEADS = 16
CAP = 2
F32 = jnp.float32
BF16 = jnp.bfloat16
MESH = pl.DeviceIdType.MESH
HIDDEN = -1e30
LANES = 128


def mm(a, b):
    return lax.dot_general(a, b, (((1,), (0,)), ((), ())), preferred_element_type=F32)


def mm_nt(a, b):
    return lax.dot_general(a, b, (((1,), (1,)), ((), ())), preferred_element_type=F32)


def mm_tn(a, b):
    return lax.dot_general(a, b, (((0,), (0,)), ((), ())), preferred_element_type=F32)


def iota(shape, axis):
    return lax.broadcasted_iota(jnp.int32, shape, axis)


def kernel(
    n,
    g,
    latent,
    feat,
    bias,
    route,
    tmask,
    wq,
    wk,
    wv,
    wo,
    gout,
    attended,
    grad_latent,
    grad_obs,
    grads,
    sbuf,
    rbuf,
    place,
    addt,
    q_s,
    qt_s,
    da_s,
    dat_s,
    k_s,
    v_s,
    kt_s,
    vt_s,
    attnt_s,
    dqt_s,
    dk_s,
    dv_s,
    dq_s,
    attn_s,
    fsend,
    frecv,
    a2a_ss,
    a2a_rs,
    ret_ss,
    ret_rs,
    rs_ss,
    rs_rs,
    z_ss,
    z_rs,
    zg_ss,
    zg_rs,
    *rest,
):
    me = lax.axis_index("band")
    mz = lax.axis_index("grp")
    lat_rows, width = latent.shape
    obs_rows = feat.shape[0]
    blocks, tiles = tmask.shape
    ob = obs_rows // blocks
    key_rows = n * CAP * ob
    part = CAP * ob
    head = width // HEADS
    scale = 1.0 / math.sqrt(head)
    chunks = width // LANES
    levels = n.bit_length() - 1
    rows = 4 * width // n
    zrows = rows // g
    two_step = zrows % 16 == 0

    term = rest[:chunks]
    pos_at = chunks
    recv = []
    acc = []
    for c in range(chunks):
        recv.append(rest[pos_at : pos_at + levels])
        pos_at += levels
        acc.append(rest[pos_at : pos_at + levels])
        pos_at += levels
    zrecv, zown, zfull = rest[pos_at : pos_at + 3]

    barrier = pltpu.get_barrier_semaphore()
    for d in range(1, n):
        pl.semaphore_signal(
            barrier, inc=1, device_id={"band": lax.rem(me + d, n)}, device_id_type=MESH
        )
    for d in range(1, g):
        pl.semaphore_signal(
            barrier, inc=1, device_id={"grp": lax.rem(mz + d, g)}, device_id_type=MESH
        )

    blk_of = iota((blocks, obs_rows), 1) // ob
    row_id = iota((blocks, obs_rows), 0)
    expand = blk_of == row_id
    route_c = jnp.broadcast_to(route[...], (blocks, obs_rows))
    route_r = jnp.sum(jnp.where(expand, route_c, 0), axis=0, keepdims=True)
    rank_r = jnp.sum(
        jnp.where((route_c == route_r) & (row_id < blk_of), 1, 0), axis=0, keepdims=True
    )
    dest = (route_r * CAP + rank_r) * ob + lax.rem(iota((1, obs_rows), 1), ob)
    hit = iota((key_rows, obs_rows), 0) == dest
    placing = jnp.where(hit, 1.0, 0.0).astype(BF16)
    place[...] = placing
    sbuf[:, :, :width] = mm(placing, feat[...]).astype(BF16).reshape(n, part, width)
    widen = jnp.where(iota((tiles, LANES), 0) == iota((tiles, LANES), 1), 1.0, 0.0).astype(BF16)
    mask_w = mm(tmask[...].astype(F32).astype(BF16), widen).astype(BF16)
    mask_o = mm_tn(jnp.where(expand, 1.0, 0.0).astype(BF16), mask_w).astype(BF16)
    bias_col = jnp.sum(jnp.where(hit, bias[...].astype(F32), 0.0), axis=1, keepdims=True)
    meta_s = mm(placing, mask_o) + jnp.where(iota((key_rows, LANES), 1) == tiles, bias_col, 0.0)
    sbuf[:, :, width:] = meta_s.astype(BF16).reshape(n, part, LANES)

    pl.semaphore_wait(barrier, n - 1 + g - 1)

    def exchange(src, dst, ss, rs):
        copies = []
        for d in range(1, n):
            peer = lax.rem(me + d, n)
            copy = pltpu.make_async_remote_copy(
                src_ref=src.at[peer],
                dst_ref=dst.at[me],
                send_sem=ss.at[d],
                recv_sem=rs.at[d],
                device_id={"band": peer},
                device_id_type=MESH,
            )
            copy.start()
            copies.append(copy)
        return copies

    a2a = exchange(sbuf, rbuf, a2a_ss, a2a_rs)
    rbuf[me] = sbuf[me]

    query = mm(latent[...], wq[...]).astype(BF16)
    q_s[...] = query
    qt_s[...] = query.T
    dattn = mm_nt(gout[...], wo[...]).astype(BF16)
    da_s[...] = dattn
    dat_s[...] = dattn.T
    dk_s[...] = jnp.zeros_like(dk_s)
    dv_s[...] = jnp.zeros_like(dv_s)

    for copy in a2a:
        copy.wait()
    got = rbuf[:, :, :width].reshape(key_rows, width)
    keys = mm(got, wk[...]).astype(BF16)
    values = mm(got, wv[...]).astype(BF16)
    k_s[...] = keys
    v_s[...] = values
    kt_s[...] = keys.T
    vt_s[...] = values.T
    meta = rbuf[:, :, width:].reshape(key_rows, LANES)
    pick = jnp.where(
        iota((LANES, lat_rows), 0) == iota((LANES, lat_rows), 1) // (lat_rows // tiles), 1.0, 0.0
    ).astype(BF16)
    bias_pick = jnp.where(iota((LANES, lat_rows), 0) == tiles, 1.0, 0.0).astype(BF16)
    addt[...] = jnp.where(mm(meta, pick) > 0.5, mm(meta, bias_pick), HIDDEN)

    gw = min(256, width)
    per_group = gw // head
    unroll = 2
    for grp_at in range(width // gw):
        cols = slice(grp_at * gw, (grp_at + 1) * gw)

        def one_head(local):
            lane_head = iota((1, gw), 1) // head
            own = jnp.where(lane_head == local, 1.0, 0.0)
            own_b = own.astype(BF16)
            start = pl.multiple_of(grp_at * gw + local * head, head)
            hrows = pl.ds(start, head)
            scores = mm(k_s[:, cols] * own_b, qt_s[cols, :]) * scale + addt[...]
            top = jnp.maximum(jnp.max(scores, axis=0, keepdims=True), 0.0)
            expo = jnp.exp(scores - top)
            total = jnp.exp(-top) + jnp.sum(expo, axis=0, keepdims=True)
            prob = expo * (1.0 / total)
            prob_b = prob.astype(BF16)
            attnt_s[hrows, :] = mm(vt_s[hrows, :], prob_b).astype(BF16)
            dprob = mm(v_s[:, cols] * own_b, dat_s[cols, :])
            delta = jnp.sum(prob * dprob, axis=0, keepdims=True)
            dscore = (prob * (dprob - delta)).astype(BF16)
            dqt_s[hrows, :] = (mm(kt_s[hrows, :], dscore) * scale).astype(BF16)
            dk_s[:, cols] += mm(dscore, q_s[:, cols]) * own
            dv_s[:, cols] += mm(prob_b, da_s[:, cols]) * own

        def pair(i, carry):
            for u in range(unroll):
                one_head(i * unroll + u)
            return carry

        lax.fori_loop(0, per_group // unroll, pair, 0)

    dkeys = (dk_s[...] * scale).astype(BF16)
    dvalues = dv_s[...].astype(BF16)
    fsend[...] = (
        (mm_nt(dkeys, wk[...]) + mm_nt(dvalues, wv[...])).astype(BF16).reshape(n, part, width)
    )
    ret = exchange(fsend, frecv, ret_ss, ret_rs)
    frecv[me] = fsend[me]

    dq_s[...] = dqt_s[...].T
    share = 1.0 / float(g)

    started = []

    def low_first(c, level):
        return level == 0 or c % 2 == 0

    def bit_of(c, level):
        if level == 0 or c % 2 == 0:
            return level
        return levels - level

    def source(c, level):
        return term[c] if level == 0 else acc[c][level - 1]

    def side(c, level, which):
        ref = source(c, level)
        if low_first(c, level):
            return ref.at[:, which]
        return ref.at[which]

    def level_copy(c, level):
        step = 1 << bit_of(c, level)
        mine = lax.rem(me // step, 2)
        partner = me + (1 - 2 * mine) * step
        return mine, pltpu.make_async_remote_copy(
            src_ref=side(c, level, 1 - mine),
            dst_ref=recv[c][level],
            send_sem=rs_ss.at[c, level],
            recv_sem=rs_rs.at[c, level],
            device_id={"band": partner},
            device_id_type=MESH,
        )

    def start_level(c, level):
        copy = level_copy(c, level)[1]
        copy.start()
        started.append(copy)

    def finish_level(c, level):
        mine, copy = level_copy(c, level)
        copy.wait_recv()
        total = (side(c, level, mine)[...].astype(F32) + recv[c][level][...].astype(F32)).astype(
            BF16
        )
        if level == levels - 1 and not two_step:
            acc[c][level][...] = total.reshape(rows, LANES)
        else:
            acc[c][level][...] = total.reshape(acc[c][level].shape)

    def z_copies(c):
        copies = []
        for d in range(1, g):
            peer = lax.rem(mz + d, g)
            full = acc[c][levels - 1]
            copies.append(
                pltpu.make_async_remote_copy(
                    src_ref=full.at[peer] if two_step else full,
                    dst_ref=zrecv.at[c, d],
                    send_sem=z_ss.at[c, d],
                    recv_sem=z_rs.at[c, d],
                    device_id={"grp": peer},
                    device_id_type=MESH,
                )
            )
        return copies

    def zg_copies(c):
        copies = []
        for d in range(1, g):
            peer = lax.rem(mz + d, g)
            copies.append(
                pltpu.make_async_remote_copy(
                    src_ref=zown.at[c],
                    dst_ref=zfull.at[c, mz],
                    send_sem=zg_ss.at[c, d],
                    recv_sem=zg_rs.at[c, d],
                    device_id={"grp": peer},
                    device_id_type=MESH,
                )
            )
        return copies

    def begin(copies):
        for copy in copies:
            copy.start()
            started.append(copy)

    def z_total(c):
        for copy in z_copies(c):
            copy.wait_recv()
        full = acc[c][levels - 1]
        total = (full[mz] if two_step else full[...]).astype(F32)
        for d in range(1, g):
            total = total + zrecv[c, d].astype(F32)
        return total

    def out_cols(c):
        return slice(c * LANES, (c + 1) * LANES)

    def event(c, level):
        if level < levels:
            finish_level(c, level)
            if level + 1 < levels:
                start_level(c, level + 1)
            else:
                begin(z_copies(c))
        elif level == levels:
            total = z_total(c)
            if two_step:
                zown[c] = total.astype(BF16)
                begin(zg_copies(c))
                zfull[c, mz] = total.astype(BF16)
            else:
                grads[:, out_cols(c)] = total
        elif two_step:
            for copy in zg_copies(c):
                copy.wait_recv()
            grads[:, out_cols(c)] = zfull[c].reshape(rows, LANES).astype(F32)

    got2 = rbuf[:, :, :width].reshape(key_rows, width)
    wave = 2
    waves = chunks // wave
    for p in range(waves):
        cols = slice(p * wave * LANES, (p + 1) * wave * LANES)
        pieces = (
            mm_tn(latent[...], dq_s[:, cols]),
            mm_tn(got2, dkeys[:, cols]),
            mm_tn(got2, dvalues[:, cols]),
            mm(attnt_s[...], gout[:, cols]),
        )
        for u in range(wave):
            c = p * wave + u
            for w, piece in enumerate(pieces):
                value = (piece[:, u * LANES : (u + 1) * LANES] * share).astype(BF16)
                term[c][w * n // 8 : (w + 1) * n // 8] = value.reshape(n // 8, 2, rows, LANES)
            start_level(c, 0)

    attn_s[...] = attnt_s[...].T
    steps = levels + 2
    for t in range(steps + waves - 1):
        for p in range(waves):
            level = t - p
            if 0 <= level < steps:
                for u in range(wave):
                    event(p * wave + u, level)
        if t == 0:
            grad_latent[...] = mm_nt(dq_s[...], wq[...]).astype(BF16)
        if t == 1:
            attended[...] = mm(attn_s[...], wo[...]).astype(BF16)
        if t == 2:
            for copy in ret:
                copy.wait()
            grad_obs[...] = mm_tn(place[...], frecv[...].reshape(key_rows, width)).astype(BF16)
    for copy in started:
        copy.wait_send()


def per_device(n, g, *args):
    latent, feat, bias, route, tmask, wq, wk, wv, wo, gout = args
    lat_rows, width = latent.shape
    obs_rows = feat.shape[0]
    blocks = route.shape[0]
    part = CAP * (obs_rows // blocks)
    key_rows = n * part
    chunks = width // LANES
    levels = n.bit_length() - 1
    rows = 4 * width // n
    two_step = (rows // g) % 16 == 0
    vm = pltpu.VMEM
    sem = pltpu.SemaphoreType.DMA
    scratch = [
        vm((n, part, width + LANES), BF16),
        vm((n, part, width + LANES), BF16),
        vm((key_rows, obs_rows), BF16),
        vm((key_rows, lat_rows), F32),
        vm((lat_rows, width), BF16),
        vm((width, lat_rows), BF16),
        vm((lat_rows, width), BF16),
        vm((width, lat_rows), BF16),
        vm((key_rows, width), BF16),
        vm((key_rows, width), BF16),
        vm((width, key_rows), BF16),
        vm((width, key_rows), BF16),
        vm((width, lat_rows), BF16),
        vm((width, lat_rows), BF16),
        vm((key_rows, width), F32),
        vm((key_rows, width), F32),
        vm((lat_rows, width), BF16),
        vm((lat_rows, width), BF16),
        vm((n, part, width), BF16),
        vm((n, part, width), BF16),
        sem((n,)),
        sem((n,)),
        sem((n,)),
        sem((n,)),
        sem((chunks, levels)),
        sem((chunks, levels)),
        sem((chunks, g)),
        sem((chunks, g)),
        sem((chunks, g)),
        sem((chunks, g)),
    ]
    scratch += [vm((n // 2, 2, rows, LANES), BF16) for _ in range(chunks)]
    for c in range(chunks):
        for level in range(levels):
            scratch.append(vm((n >> (level + 1), rows, LANES), BF16))
        for level in range(levels):
            m = n >> (level + 1)
            if level == levels - 1:
                shape = (g, rows // g, LANES) if two_step else (rows, LANES)
            elif c % 2 == 0:
                shape = (m // 2, 2, rows, LANES)
            else:
                shape = (2, m // 2, rows, LANES)
            scratch.append(vm(shape, BF16))
    zr = rows // g if two_step else rows
    scratch.append(vm((chunks, g, zr, LANES), BF16))
    scratch.append(vm((chunks, zr, LANES), BF16))
    scratch.append(vm((chunks, g, zr, LANES), BF16))
    spec = pl.BlockSpec(memory_space=pltpu.VMEM)
    return pl.pallas_call(
        functools.partial(kernel, n, g),
        out_shape=(
            jax.ShapeDtypeStruct((lat_rows, width), BF16),
            jax.ShapeDtypeStruct((lat_rows, width), BF16),
            jax.ShapeDtypeStruct((obs_rows, width), BF16),
            jax.ShapeDtypeStruct((rows, width), F32),
        ),
        in_specs=[spec] * 10,
        out_specs=(spec,) * 4,
        scratch_shapes=scratch,
        compiler_params=pltpu.CompilerParams(
            collective_id=0, has_side_effects=True, vmem_limit_bytes=60 * 1024 * 1024
        ),
        name="fused_layer",
    )(latent, feat, bias.reshape(1, obs_rows), route, tmask, wq, wk, wv, wo, gout)


def solution(mesh):
    n = mesh.shape["band"]
    g = mesh.shape["grp"]
    return jax.shard_map(
        functools.partial(per_device, n, g),
        mesh=mesh,
        in_specs=(
            P(("grp", "band"), None),
            P(("grp", "band"), None),
            P(("grp", "band")),
            P(("grp", "band"), None),
            P(("grp", "band"), None),
            P(),
            P(),
            P(),
            P(),
            P(("grp", "band"), None),
        ),
        out_specs=(
            P(("grp", "band"), None),
            P(("grp", "band"), None),
            P(("grp", "band"), None),
            P("band", None),
        ),
        check_vma=False,
    )
```

```python
import functools
import math

import jax
import jax.numpy as jnp
from jax import lax
from jax.experimental import pallas as pl
from jax.experimental.pallas import tpu as pltpu
from jax.sharding import PartitionSpec as P

HEADS = 16
CAP = 2
F32 = jnp.float32
BF16 = jnp.bfloat16
MESH = pl.DeviceIdType.MESH
HIDDEN = -1e30
LANES = 128


def mm(a, b):
    return lax.dot_general(a, b, (((1,), (0,)), ((), ())), preferred_element_type=F32)


def mm_nt(a, b):
    return lax.dot_general(a, b, (((1,), (1,)), ((), ())), preferred_element_type=F32)


def mm_tn(a, b):
    return lax.dot_general(a, b, (((0,), (0,)), ((), ())), preferred_element_type=F32)


def iota(shape, axis):
    return lax.broadcasted_iota(jnp.int32, shape, axis)


def kernel(
    n,
    g,
    latent_h,
    feat_h,
    bias,
    route,
    tmask,
    wq_h,
    wk_h,
    wv_h,
    wo_h,
    gout_h,
    attended,
    grad_latent,
    grad_obs,
    grads,
    latent,
    feat,
    wq,
    wk,
    wv,
    wo,
    gout,
    in_sem,
    latt_s,
    gott_s,
    prob_s,
    sbuf,
    rbuf,
    place,
    addt,
    q_s,
    qt_s,
    da_s,
    dat_s,
    k_s,
    v_s,
    kt_s,
    vt_s,
    attnt_s,
    dqt_s,
    dk_s,
    dv_s,
    dq_s,
    attn_s,
    fsend,
    frecv,
    a2a_ss,
    a2a_rs,
    ret_ss,
    ret_rs,
    rs_ss,
    rs_rs,
    z_ss,
    z_rs,
    zg_ss,
    zg_rs,
    *rest,
):
    me = lax.axis_index("band")
    mz = lax.axis_index("grp")
    lat_rows, width = latent.shape
    obs_rows = feat.shape[0]
    tiles, blocks = tmask.shape
    ob = obs_rows // blocks
    key_rows = n * CAP * ob
    part = CAP * ob
    head = width // HEADS
    scale = 1.0 / math.sqrt(head)
    chunks = width // LANES
    levels = n.bit_length() - 1
    rows = 4 * width // n
    zrows = rows // g
    two_step = zrows % 16 == 0

    term = rest[:chunks]
    pos_at = chunks
    recv = []
    acc = []
    for c in range(chunks):
        recv.append(rest[pos_at : pos_at + levels])
        pos_at += levels
        acc.append(rest[pos_at : pos_at + levels])
        pos_at += levels
    zrecv, zown, zfull = rest[pos_at : pos_at + 3]

    pairs = (
        (feat_h, feat),
        (latent_h, latent),
        (wq_h, wq),
        (gout_h, gout),
        (wo_h, wo),
        (wk_h, wk),
        (wv_h, wv),
    )
    loads = [pltpu.make_async_copy(a, b, in_sem.at[i]) for i, (a, b) in enumerate(pairs)]
    for load in loads:
        load.start()
    barrier = pltpu.get_barrier_semaphore()
    for d in range(1, n):
        pl.semaphore_signal(
            barrier, inc=1, device_id={"band": lax.rem(me + d, n)}, device_id_type=MESH
        )
    for d in range(1, g):
        pl.semaphore_signal(
            barrier, inc=1, device_id={"grp": lax.rem(mz + d, g)}, device_id_type=MESH
        )

    blk_of = iota((blocks, obs_rows), 1) // ob
    row_id = iota((blocks, obs_rows), 0)
    expand = blk_of == row_id
    expand_b = jnp.where(expand, 1.0, 0.0).astype(BF16)
    diagonal = iota((blocks, blocks), 0) == iota((blocks, blocks), 1)
    route_d = jnp.where(diagonal, route[...].astype(F32), 0.0).astype(BF16)
    route_c = mm(route_d, jnp.ones((blocks, obs_rows), BF16)).astype(jnp.int32)
    route_r = jnp.sum(jnp.where(expand, route_c, 0), axis=0, keepdims=True)
    rank_r = jnp.sum(
        jnp.where((route_c == route_r) & (row_id < blk_of), 1, 0), axis=0, keepdims=True
    )
    dest = (route_r * CAP + rank_r) * ob + lax.rem(iota((1, obs_rows), 1), ob)
    hit = iota((key_rows, obs_rows), 0) == dest
    placing = jnp.where(hit, 1.0, 0.0).astype(BF16)
    place[...] = placing
    loads[0].wait()
    sbuf[:, :, :width] = mm(placing, feat[...]).astype(BF16).reshape(n, part, width)
    widen = jnp.where(iota((tiles, LANES), 0) == iota((tiles, LANES), 1), 1.0, 0.0).astype(BF16)
    mask_w = mm_tn(tmask[...].astype(F32).astype(BF16), widen).astype(BF16)
    mask_o = mm_tn(expand_b, mask_w).astype(BF16)
    bias_col = jnp.sum(jnp.where(hit, bias[...].astype(F32), 0.0), axis=1, keepdims=True)
    meta_s = mm(placing, mask_o) + jnp.where(iota((key_rows, LANES), 1) == tiles, bias_col, 0.0)
    sbuf[:, :, width:] = meta_s.astype(BF16).reshape(n, part, LANES)

    pl.semaphore_wait(barrier, n - 1 + g - 1)

    def exchange(src, dst, ss, rs):
        copies = []
        for d in range(1, n):
            peer = lax.rem(me + d, n)
            copy = pltpu.make_async_remote_copy(
                src_ref=src.at[peer],
                dst_ref=dst.at[me],
                send_sem=ss.at[d],
                recv_sem=rs.at[d],
                device_id={"band": peer},
                device_id_type=MESH,
            )
            copy.start()
            copies.append(copy)
        return copies

    a2a = exchange(sbuf, rbuf, a2a_ss, a2a_rs)
    rbuf[me] = sbuf[me]

    loads[1].wait()
    loads[2].wait()
    query = mm(latent[...], wq[...]).astype(BF16)
    q_s[...] = query
    qt_s[...] = query.T
    loads[3].wait()
    loads[4].wait()
    dattn = mm_nt(gout[...], wo[...]).astype(BF16)
    da_s[...] = dattn
    dat_s[...] = dattn.T
    latt_s[...] = latent[...].T
    dk_s[...] = jnp.zeros_like(dk_s)
    dv_s[...] = jnp.zeros_like(dv_s)

    loads[5].wait()
    loads[6].wait()
    for copy in a2a:
        copy.wait()
    got = rbuf[:, :, :width].reshape(key_rows, width)
    gott_s[...] = got.T
    keys = mm(got, wk[...]).astype(BF16)
    values = mm(got, wv[...]).astype(BF16)
    k_s[...] = keys
    v_s[...] = values
    kt_s[...] = keys.T
    vt_s[...] = values.T
    meta = rbuf[:, :, width:].reshape(key_rows, LANES)
    pick = jnp.where(
        iota((LANES, lat_rows), 0) == iota((LANES, lat_rows), 1) // (lat_rows // tiles), 1.0, 0.0
    ).astype(BF16)
    bias_pick = jnp.where(iota((LANES, lat_rows), 0) == tiles, 1.0, 0.0).astype(BF16)
    addt[...] = jnp.where(mm(meta, pick) > 0.5, mm(meta, bias_pick), HIDDEN)

    gw = min(256, width)
    per_group = gw // head
    unroll = 2
    heads_per_chunk = LANES // head

    def place_of(grp_at, local):
        own = jnp.where(iota((1, gw), 1) // head == local, 1.0, 0.0)
        start = pl.multiple_of(grp_at * gw + local * head, head)
        return own, pl.ds(start, head)

    for grp_at in range(width // gw):

        def forward(local, grp_at=grp_at):
            cols = slice(grp_at * gw, (grp_at + 1) * gw)
            own, hrows = place_of(grp_at, local)
            scores = mm(k_s[:, cols] * own.astype(BF16), qt_s[cols, :]) * scale + addt[...]
            top = jnp.maximum(jnp.max(scores, axis=0, keepdims=True), 0.0)
            expo = jnp.exp(scores - top)
            total = jnp.exp(-top) + jnp.sum(expo, axis=0, keepdims=True)
            prob = expo * (1.0 / total)
            prob_s[grp_at * per_group + local] = prob
            attnt_s[hrows, :] = mm(vt_s[hrows, :], prob.astype(BF16)).astype(BF16)

        def forwards(i, carry, forward=forward):
            for u in range(unroll):
                forward(i * unroll + u)
            return carry

        lax.fori_loop(0, per_group // unroll, forwards, 0)

    def backward(grp_at, local):
        cols = slice(grp_at * gw, (grp_at + 1) * gw)
        own, hrows = place_of(grp_at, local)
        prob = prob_s[grp_at * per_group + local]
        dprob = mm(v_s[:, cols] * own.astype(BF16), dat_s[cols, :])
        delta = jnp.sum(prob * dprob, axis=0, keepdims=True)
        dscore = (prob * (dprob - delta)).astype(BF16)
        dqt_s[hrows, :] = (mm(kt_s[hrows, :], dscore) * scale).astype(BF16)
        dk_s[:, cols] += mm(dscore, q_s[:, cols]) * own
        dv_s[:, cols] += mm(prob.astype(BF16), da_s[:, cols]) * own

    def backward_chunk(c):
        grp_at = c * LANES // gw
        first = (c * LANES - grp_at * gw) // head

        def backwards(i, carry):
            for u in range(unroll):
                backward(grp_at, first + i * unroll + u)
            return carry

        lax.fori_loop(0, heads_per_chunk // unroll, backwards, 0)

    share = 1.0 / float(g)

    started = []

    def low_first(c, level):
        return level == 0 or c % 2 == 0

    def bit_of(c, level):
        if level == 0 or c % 2 == 0:
            return level
        return levels - level

    def source(c, level):
        return term[c] if level == 0 else acc[c][level - 1]

    def side(c, level, which):
        ref = source(c, level)
        if low_first(c, level):
            return ref.at[:, which]
        return ref.at[which]

    def level_copy(c, level):
        step = 1 << bit_of(c, level)
        mine = lax.rem(me // step, 2)
        partner = me + (1 - 2 * mine) * step
        return mine, pltpu.make_async_remote_copy(
            src_ref=side(c, level, 1 - mine),
            dst_ref=recv[c][level],
            send_sem=rs_ss.at[c, level],
            recv_sem=rs_rs.at[c, level],
            device_id={"band": partner},
            device_id_type=MESH,
        )

    def start_level(c, level):
        copy = level_copy(c, level)[1]
        copy.start()
        started.append(copy)

    def finish_level(c, level):
        mine, copy = level_copy(c, level)
        copy.wait_recv()
        total = (side(c, level, mine)[...].astype(F32) + recv[c][level][...].astype(F32)).astype(
            BF16
        )
        if level == levels - 1 and not two_step:
            acc[c][level][...] = total.reshape(rows, LANES)
        else:
            acc[c][level][...] = total.reshape(acc[c][level].shape)

    def z_copies(c):
        copies = []
        for d in range(1, g):
            peer = lax.rem(mz + d, g)
            full = acc[c][levels - 1]
            copies.append(
                pltpu.make_async_remote_copy(
                    src_ref=full.at[peer] if two_step else full,
                    dst_ref=zrecv.at[c, d],
                    send_sem=z_ss.at[c, d],
                    recv_sem=z_rs.at[c, d],
                    device_id={"grp": peer},
                    device_id_type=MESH,
                )
            )
        return copies

    def zg_copies(c):
        copies = []
        for d in range(1, g):
            peer = lax.rem(mz + d, g)
            copies.append(
                pltpu.make_async_remote_copy(
                    src_ref=zown.at[c],
                    dst_ref=zfull.at[c, mz],
                    send_sem=zg_ss.at[c, d],
                    recv_sem=zg_rs.at[c, d],
                    device_id={"grp": peer},
                    device_id_type=MESH,
                )
            )
        return copies

    def begin(copies):
        for copy in copies:
            copy.start()
            started.append(copy)

    def z_total(c):
        for copy in z_copies(c):
            copy.wait_recv()
        full = acc[c][levels - 1]
        total = (full[mz] if two_step else full[...]).astype(F32)
        for d in range(1, g):
            total = total + zrecv[c, d].astype(F32)
        return total

    def out_cols(c):
        return slice(c * LANES, (c + 1) * LANES)

    def event(c, level):
        if level < levels:
            finish_level(c, level)
            if level + 1 < levels:
                start_level(c, level + 1)
            else:
                begin(z_copies(c))
        elif level == levels:
            total = z_total(c)
            if two_step:
                zown[c] = total.astype(BF16)
                begin(zg_copies(c))
                zfull[c, mz] = total.astype(BF16)
            else:
                grads[:, out_cols(c)] = total
        elif two_step:
            for copy in zg_copies(c):
                copy.wait_recv()
            grads[:, out_cols(c)] = zfull[c].reshape(rows, LANES).astype(F32)

    steps = levels + 2

    def events(t):
        for c in range(chunks):
            level = t - c - 1
            if 0 <= level < steps:
                event(c, level)

    for c in range(chunks):
        backward_chunk(c)
        cols = out_cols(c)
        dq = dqt_s[cols, :].T
        dq_s[:, cols] = dq
        pieces = (
            mm(latt_s[...], dq),
            mm(gott_s[...], (dk_s[:, cols] * scale).astype(BF16)),
            mm(gott_s[...], dv_s[:, cols].astype(BF16)),
            mm(attnt_s[...], gout[:, cols]),
        )
        for w, piece in enumerate(pieces):
            value = (piece * share).astype(BF16)
            term[c][w * n // 8 : (w + 1) * n // 8] = value.reshape(n // 8, 2, rows, LANES)
        start_level(c, 0)
        events(c)

    dkeys = (dk_s[...] * scale).astype(BF16)
    dvalues = dv_s[...].astype(BF16)
    fsend[...] = (
        (mm_nt(dkeys, wk[...]) + mm_nt(dvalues, wv[...])).astype(BF16).reshape(n, part, width)
    )
    ret = exchange(fsend, frecv, ret_ss, ret_rs)
    frecv[me] = fsend[me]
    for t in range(chunks, steps + chunks):
        events(t)
        if t == chunks:
            grad_latent[...] = mm_nt(dq_s[...], wq[...]).astype(BF16)
        if t == chunks + 1:
            attn_s[...] = attnt_s[...].T
            attended[...] = mm(attn_s[...], wo[...]).astype(BF16)
        if t == chunks + 2:
            for copy in ret:
                copy.wait()
            grad_obs[...] = mm_tn(place[...], frecv[...].reshape(key_rows, width)).astype(BF16)
    for copy in started:
        copy.wait_send()


def move(*refs):
    k = len(refs) // 3
    ins, outs, bufs = refs[:k], refs[k : 2 * k], refs[2 * k : 3 * k]
    in_sem, out_sem = refs[3 * k :]
    loads = [pltpu.make_async_copy(ins[i], bufs[i], in_sem.at[i]) for i in range(k)]
    stores = [pltpu.make_async_copy(bufs[i], outs[i], out_sem.at[i]) for i in range(k)]
    for load in loads:
        load.start()
    for load, store in zip(loads, stores):
        load.wait()
        store.start()
    for store in stores:
        store.wait()


def hand_out(results):
    far = pl.BlockSpec(memory_space=pltpu.HBM)
    k = len(results)
    return pl.pallas_call(
        move,
        out_shape=tuple(jax.ShapeDtypeStruct(r.shape, r.dtype) for r in results),
        in_specs=[far] * k,
        out_specs=(far,) * k,
        scratch_shapes=[pltpu.VMEM(r.shape, r.dtype) for r in results]
        + [pltpu.SemaphoreType.DMA((k,)), pltpu.SemaphoreType.DMA((k,))],
        compiler_params=pltpu.CompilerParams(vmem_limit_bytes=60 * 1024 * 1024),
        name="hand_out",
    )(*results)


def per_device(n, g, *args):
    latent, feat, bias, route, tmask, wq, wk, wv, wo, gout = args
    lat_rows, width = latent.shape
    obs_rows = feat.shape[0]
    blocks, tiles = tmask.shape
    part = CAP * (obs_rows // blocks)
    key_rows = n * part
    chunks = width // LANES
    levels = n.bit_length() - 1
    rows = 4 * width // n
    two_step = (rows // g) % 16 == 0
    vm = pltpu.VMEM
    sem = pltpu.SemaphoreType.DMA
    weight = vm((width, width), BF16)
    scratch = [
        vm((lat_rows, width), BF16),
        vm((obs_rows, width), BF16),
        weight,
        weight,
        weight,
        weight,
        vm((lat_rows, width), BF16),
        sem((7,)),
        vm((width, lat_rows), BF16),
        vm((width, key_rows), BF16),
        vm((HEADS, key_rows, lat_rows), F32),
        vm((n, part, width + LANES), BF16),
        vm((n, part, width + LANES), BF16),
        vm((key_rows, obs_rows), BF16),
        vm((key_rows, lat_rows), F32),
        vm((lat_rows, width), BF16),
        vm((width, lat_rows), BF16),
        vm((lat_rows, width), BF16),
        vm((width, lat_rows), BF16),
        vm((key_rows, width), BF16),
        vm((key_rows, width), BF16),
        vm((width, key_rows), BF16),
        vm((width, key_rows), BF16),
        vm((width, lat_rows), BF16),
        vm((width, lat_rows), BF16),
        vm((key_rows, width), F32),
        vm((key_rows, width), F32),
        vm((lat_rows, width), BF16),
        vm((lat_rows, width), BF16),
        vm((n, part, width), BF16),
        vm((n, part, width), BF16),
        sem((n,)),
        sem((n,)),
        sem((n,)),
        sem((n,)),
        sem((chunks, levels)),
        sem((chunks, levels)),
        sem((chunks, g)),
        sem((chunks, g)),
        sem((chunks, g)),
        sem((chunks, g)),
    ]
    scratch += [vm((n // 2, 2, rows, LANES), BF16) for _ in range(chunks)]
    for c in range(chunks):
        for level in range(levels):
            scratch.append(vm((n >> (level + 1), rows, LANES), BF16))
        for level in range(levels):
            m = n >> (level + 1)
            if level == levels - 1:
                shape = (g, rows // g, LANES) if two_step else (rows, LANES)
            elif c % 2 == 0:
                shape = (m // 2, 2, rows, LANES)
            else:
                shape = (2, m // 2, rows, LANES)
            scratch.append(vm(shape, BF16))
    zr = rows // g if two_step else rows
    scratch.append(vm((chunks, g, zr, LANES), BF16))
    scratch.append(vm((chunks, zr, LANES), BF16))
    scratch.append(vm((chunks, g, zr, LANES), BF16))
    spec = pl.BlockSpec(memory_space=pltpu.VMEM)
    far = pl.BlockSpec(memory_space=pltpu.HBM)
    results = pl.pallas_call(
        functools.partial(kernel, n, g),
        out_shape=(
            jax.ShapeDtypeStruct((lat_rows, width), BF16),
            jax.ShapeDtypeStruct((lat_rows, width), BF16),
            jax.ShapeDtypeStruct((obs_rows, width), BF16),
            jax.ShapeDtypeStruct((rows, width), F32),
        ),
        in_specs=[far, far, spec, spec, spec, far, far, far, far, far],
        out_specs=(spec,) * 4,
        scratch_shapes=scratch,
        compiler_params=pltpu.CompilerParams(
            collective_id=0, has_side_effects=True, vmem_limit_bytes=60 * 1024 * 1024
        ),
        name="fused_layer",
    )(latent, feat, bias.reshape(1, obs_rows), route.T, tmask.T, wq, wk, wv, wo, gout)
    return hand_out(results)


def solution(mesh):
    n = mesh.shape["band"]
    g = mesh.shape["grp"]
    return jax.shard_map(
        functools.partial(per_device, n, g),
        mesh=mesh,
        in_specs=(
            P(("grp", "band"), None),
            P(("grp", "band"), None),
            P(("grp", "band")),
            P(("grp", "band"), None),
            P(("grp", "band"), None),
            P(),
            P(),
            P(),
            P(),
            P(("grp", "band"), None),
        ),
        out_specs=(
            P(("grp", "band"), None),
            P(("grp", "band"), None),
            P(("grp", "band"), None),
            P("band", None),
        ),
        check_vma=False,
    )
```

```python
import functools
import math

import jax
import jax.numpy as jnp
from jax import lax
from jax.experimental import pallas as pl
from jax.experimental.pallas import tpu as pltpu
from jax.sharding import PartitionSpec as P

HEADS = 16
CAP = 2
F32 = jnp.float32
BF16 = jnp.bfloat16
MESH = pl.DeviceIdType.MESH
HIDDEN = -1e30
LANES = 128


def mm(a, b):
    return lax.dot_general(a, b, (((1,), (0,)), ((), ())), preferred_element_type=F32)


def mm_nt(a, b):
    return lax.dot_general(a, b, (((1,), (1,)), ((), ())), preferred_element_type=F32)


def mm_tn(a, b):
    return lax.dot_general(a, b, (((0,), (0,)), ((), ())), preferred_element_type=F32)


def iota(shape, axis):
    return lax.broadcasted_iota(jnp.int32, shape, axis)


def kernel(
    n,
    g,
    latent_h,
    feat_h,
    bias,
    route,
    tmask,
    wq_h,
    wk_h,
    wv_h,
    wo_h,
    gout_h,
    attended,
    grad_latent,
    grad_obs,
    grads,
    latent,
    feat,
    wq,
    wk,
    wv,
    wo,
    gout,
    in_sem,
    latt_s,
    gott_s,
    prob_s,
    sbuf,
    rbuf,
    place,
    addt,
    q_s,
    qt_s,
    da_s,
    dat_s,
    k_s,
    v_s,
    kt_s,
    vt_s,
    attnt_s,
    dqt_s,
    dk_s,
    dv_s,
    dq_s,
    attn_s,
    fsend,
    frecv,
    a2a_ss,
    a2a_rs,
    ret_ss,
    ret_rs,
    rs_ss,
    rs_rs,
    z_ss,
    z_rs,
    zg_ss,
    zg_rs,
    *rest,
):
    me = lax.axis_index("band")
    mz = lax.axis_index("grp")
    lat_rows, width = latent.shape
    obs_rows = feat.shape[0]
    tiles, blocks = tmask.shape
    ob = obs_rows // blocks
    key_rows = n * CAP * ob
    part = CAP * ob
    head = width // HEADS
    scale = 1.0 / math.sqrt(head)
    chunks = width // LANES
    levels = n.bit_length() - 1
    rows = 4 * width // n
    zrows = rows // g
    two_step = zrows % 16 == 0

    term = rest[:chunks]
    pos_at = chunks
    recv = []
    acc = []
    for c in range(chunks):
        recv.append(rest[pos_at : pos_at + levels])
        pos_at += levels
        acc.append(rest[pos_at : pos_at + levels])
        pos_at += levels
    zrecv, zown, zfull = rest[pos_at : pos_at + 3]

    pairs = (
        (feat_h, feat),
        (latent_h, latent),
        (wq_h, wq),
        (gout_h, gout),
        (wo_h, wo),
        (wk_h, wk),
        (wv_h, wv),
    )
    loads = [pltpu.make_async_copy(a, b, in_sem.at[i]) for i, (a, b) in enumerate(pairs)]
    for load in loads:
        load.start()
    barrier = pltpu.get_barrier_semaphore()
    for d in range(1, n):
        pl.semaphore_signal(
            barrier, inc=1, device_id={"band": lax.rem(me + d, n)}, device_id_type=MESH
        )
    for d in range(1, g):
        pl.semaphore_signal(
            barrier, inc=1, device_id={"grp": lax.rem(mz + d, g)}, device_id_type=MESH
        )

    blk_of = iota((blocks, obs_rows), 1) // ob
    row_id = iota((blocks, obs_rows), 0)
    expand = blk_of == row_id
    expand_b = jnp.where(expand, 1.0, 0.0).astype(BF16)
    diagonal = iota((blocks, blocks), 0) == iota((blocks, blocks), 1)
    route_d = jnp.where(diagonal, route[...].astype(F32), 0.0).astype(BF16)
    route_c = mm(route_d, jnp.ones((blocks, obs_rows), BF16)).astype(jnp.int32)
    route_r = jnp.sum(jnp.where(expand, route_c, 0), axis=0, keepdims=True)
    rank_r = jnp.sum(
        jnp.where((route_c == route_r) & (row_id < blk_of), 1, 0), axis=0, keepdims=True
    )
    dest = (route_r * CAP + rank_r) * ob + lax.rem(iota((1, obs_rows), 1), ob)
    hit = iota((key_rows, obs_rows), 0) == dest
    placing = jnp.where(hit, 1.0, 0.0).astype(BF16)
    place[...] = placing
    loads[0].wait()
    sbuf[:, :, :width] = mm(placing, feat[...]).astype(BF16).reshape(n, part, width)
    widen = jnp.where(iota((tiles, LANES), 0) == iota((tiles, LANES), 1), 1.0, 0.0).astype(BF16)
    mask_w = mm_tn(tmask[...].astype(F32).astype(BF16), widen).astype(BF16)
    mask_o = mm_tn(expand_b, mask_w).astype(BF16)
    bias_col = jnp.sum(jnp.where(hit, bias[...].astype(F32), 0.0), axis=1, keepdims=True)
    meta_s = mm(placing, mask_o) + jnp.where(iota((key_rows, LANES), 1) == tiles, bias_col, 0.0)
    sbuf[:, :, width:] = meta_s.astype(BF16).reshape(n, part, LANES)

    pl.semaphore_wait(barrier, n - 1 + g - 1)

    def exchange(src, dst, ss, rs):
        copies = []
        for d in range(1, n):
            peer = lax.rem(me + d, n)
            copy = pltpu.make_async_remote_copy(
                src_ref=src.at[peer],
                dst_ref=dst.at[me],
                send_sem=ss.at[d],
                recv_sem=rs.at[d],
                device_id={"band": peer},
                device_id_type=MESH,
            )
            copy.start()
            copies.append(copy)
        return copies

    a2a = exchange(sbuf, rbuf, a2a_ss, a2a_rs)
    rbuf[me] = sbuf[me]

    loads[1].wait()
    loads[2].wait()
    query = mm(latent[...], wq[...]).astype(BF16)
    q_s[...] = query
    qt_s[...] = query.T
    loads[3].wait()
    loads[4].wait()
    dattn = mm_nt(gout[...], wo[...]).astype(BF16)
    da_s[...] = dattn
    dat_s[...] = dattn.T
    latt_s[...] = latent[...].T
    dk_s[...] = jnp.zeros_like(dk_s)
    dv_s[...] = jnp.zeros_like(dv_s)

    loads[5].wait()
    loads[6].wait()
    for copy in a2a:
        copy.wait()
    got = rbuf[:, :, :width].reshape(key_rows, width)
    gott_s[...] = got.T
    keys = mm(got, wk[...]).astype(BF16)
    values = mm(got, wv[...]).astype(BF16)
    k_s[...] = keys
    v_s[...] = values
    kt_s[...] = keys.T
    vt_s[...] = values.T
    meta = rbuf[:, :, width:].reshape(key_rows, LANES)
    pick = jnp.where(
        iota((LANES, lat_rows), 0) == iota((LANES, lat_rows), 1) // (lat_rows // tiles), 1.0, 0.0
    ).astype(BF16)
    bias_pick = jnp.where(iota((LANES, lat_rows), 0) == tiles, 1.0, 0.0).astype(BF16)
    addt[...] = jnp.where(mm(meta, pick) > 0.5, mm(meta, bias_pick), HIDDEN)

    gw = min(256, width)
    per_group = gw // head
    unroll = 4
    heads_per_chunk = LANES // head

    def place_of(grp_at, local):
        own = jnp.where(iota((1, gw), 1) // head == local, 1.0, 0.0)
        start = pl.multiple_of(grp_at * gw + local * head, head)
        return own, pl.ds(start, head)

    for grp_at in range(width // gw):

        def forward(local, grp_at=grp_at):
            cols = slice(grp_at * gw, (grp_at + 1) * gw)
            own, hrows = place_of(grp_at, local)
            scores = mm(k_s[:, cols] * own.astype(BF16), qt_s[cols, :]) * scale + addt[...]
            top = jnp.maximum(jnp.max(scores, axis=0, keepdims=True), 0.0)
            expo = jnp.exp(scores - top)
            total = jnp.exp(-top) + jnp.sum(expo, axis=0, keepdims=True)
            prob = expo * (1.0 / total)
            prob_s[grp_at * per_group + local] = prob
            attnt_s[hrows, :] = mm(vt_s[hrows, :], prob.astype(BF16)).astype(BF16)

        def forwards(i, carry, forward=forward):
            for u in range(unroll):
                forward(i * unroll + u)
            return carry

        lax.fori_loop(0, per_group // unroll, forwards, 0)

    def backward(grp_at, local):
        cols = slice(grp_at * gw, (grp_at + 1) * gw)
        own, hrows = place_of(grp_at, local)
        prob = prob_s[grp_at * per_group + local]
        dprob = mm(v_s[:, cols] * own.astype(BF16), dat_s[cols, :])
        delta = jnp.sum(prob * dprob, axis=0, keepdims=True)
        dscore = (prob * (dprob - delta)).astype(BF16)
        dqt_s[hrows, :] = (mm(kt_s[hrows, :], dscore) * scale).astype(BF16)
        dk_s[:, cols] += mm(dscore, q_s[:, cols]) * own
        dv_s[:, cols] += mm(prob.astype(BF16), da_s[:, cols]) * own

    def backward_chunk(c):
        grp_at = c * LANES // gw
        first = (c * LANES - grp_at * gw) // head

        def backwards(i, carry):
            for u in range(unroll):
                backward(grp_at, first + i * unroll + u)
            return carry

        lax.fori_loop(0, heads_per_chunk // unroll, backwards, 0)

    share = 1.0 / float(g)

    started = []

    def low_first(c, level):
        return level == 0 or c % 2 == 0

    def bit_of(c, level):
        if level == 0 or c % 2 == 0:
            return level
        return levels - level

    def source(c, level):
        return term[c] if level == 0 else acc[c][level - 1]

    def side(c, level, which):
        ref = source(c, level)
        if low_first(c, level):
            return ref.at[:, which]
        return ref.at[which]

    def level_copy(c, level):
        step = 1 << bit_of(c, level)
        mine = lax.rem(me // step, 2)
        partner = me + (1 - 2 * mine) * step
        return mine, pltpu.make_async_remote_copy(
            src_ref=side(c, level, 1 - mine),
            dst_ref=recv[c][level],
            send_sem=rs_ss.at[c, level],
            recv_sem=rs_rs.at[c, level],
            device_id={"band": partner},
            device_id_type=MESH,
        )

    def start_level(c, level):
        copy = level_copy(c, level)[1]
        copy.start()
        started.append(copy)

    def finish_level(c, level):
        mine, copy = level_copy(c, level)
        copy.wait_recv()
        total = (side(c, level, mine)[...].astype(F32) + recv[c][level][...].astype(F32)).astype(
            BF16
        )
        if level == levels - 1 and not two_step:
            acc[c][level][...] = total.reshape(rows, LANES)
        else:
            acc[c][level][...] = total.reshape(acc[c][level].shape)

    def z_copies(c):
        copies = []
        for d in range(1, g):
            peer = lax.rem(mz + d, g)
            full = acc[c][levels - 1]
            copies.append(
                pltpu.make_async_remote_copy(
                    src_ref=full.at[peer] if two_step else full,
                    dst_ref=zrecv.at[c, d],
                    send_sem=z_ss.at[c, d],
                    recv_sem=z_rs.at[c, d],
                    device_id={"grp": peer},
                    device_id_type=MESH,
                )
            )
        return copies

    def zg_copies(c):
        copies = []
        for d in range(1, g):
            peer = lax.rem(mz + d, g)
            copies.append(
                pltpu.make_async_remote_copy(
                    src_ref=zown.at[c],
                    dst_ref=zfull.at[c, mz],
                    send_sem=zg_ss.at[c, d],
                    recv_sem=zg_rs.at[c, d],
                    device_id={"grp": peer},
                    device_id_type=MESH,
                )
            )
        return copies

    def begin(copies):
        for copy in copies:
            copy.start()
            started.append(copy)

    def z_total(c):
        for copy in z_copies(c):
            copy.wait_recv()
        full = acc[c][levels - 1]
        total = (full[mz] if two_step else full[...]).astype(F32)
        for d in range(1, g):
            total = total + zrecv[c, d].astype(F32)
        return total

    def out_cols(c):
        return slice(c * LANES, (c + 1) * LANES)

    def event(c, level):
        if level < levels:
            finish_level(c, level)
            if level + 1 < levels:
                start_level(c, level + 1)
            else:
                begin(z_copies(c))
        elif level == levels:
            total = z_total(c)
            if two_step:
                zown[c] = total.astype(BF16)
                begin(zg_copies(c))
                zfull[c, mz] = total.astype(BF16)
            else:
                grads[:, out_cols(c)] = total
        elif two_step:
            for copy in zg_copies(c):
                copy.wait_recv()
            grads[:, out_cols(c)] = zfull[c].reshape(rows, LANES).astype(F32)

    steps = levels + 2

    def events(t):
        for c in range(chunks):
            level = t - c - 1
            if 0 <= level < steps:
                event(c, level)

    for c in range(chunks):
        backward_chunk(c)
        cols = out_cols(c)
        dq = dqt_s[cols, :].T
        dq_s[:, cols] = dq
        pieces = (
            mm(latt_s[...], dq),
            mm(gott_s[...], (dk_s[:, cols] * scale).astype(BF16)),
            mm(gott_s[...], dv_s[:, cols].astype(BF16)),
            mm(attnt_s[...], gout[:, cols]),
        )
        for w, piece in enumerate(pieces):
            value = (piece * share).astype(BF16)
            term[c][w * n // 8 : (w + 1) * n // 8] = value.reshape(n // 8, 2, rows, LANES)
        start_level(c, 0)
        events(c)

    dkeys = (dk_s[...] * scale).astype(BF16)
    dvalues = dv_s[...].astype(BF16)
    fsend[...] = (
        (mm_nt(dkeys, wk[...]) + mm_nt(dvalues, wv[...])).astype(BF16).reshape(n, part, width)
    )
    ret = exchange(fsend, frecv, ret_ss, ret_rs)
    frecv[me] = fsend[me]
    for t in range(chunks, steps + chunks):
        events(t)
        if t == chunks:
            grad_latent[...] = mm_nt(dq_s[...], wq[...]).astype(BF16)
        if t == chunks + 1:
            attn_s[...] = attnt_s[...].T
            attended[...] = mm(attn_s[...], wo[...]).astype(BF16)
        if t == chunks + 2:
            for copy in ret:
                copy.wait()
            grad_obs[...] = mm_tn(place[...], frecv[...].reshape(key_rows, width)).astype(BF16)
    for copy in started:
        copy.wait_send()


def move(*refs):
    k = len(refs) // 3
    ins, outs, bufs = refs[:k], refs[k : 2 * k], refs[2 * k : 3 * k]
    in_sem, out_sem = refs[3 * k :]
    loads = [pltpu.make_async_copy(ins[i], bufs[i], in_sem.at[i]) for i in range(k)]
    stores = [pltpu.make_async_copy(bufs[i], outs[i], out_sem.at[i]) for i in range(k)]
    for load in loads:
        load.start()
    for load, store in zip(loads, stores):
        load.wait()
        store.start()
    for store in stores:
        store.wait()


def hand_out(results):
    far = pl.BlockSpec(memory_space=pltpu.HBM)
    k = len(results)
    return pl.pallas_call(
        move,
        out_shape=tuple(jax.ShapeDtypeStruct(r.shape, r.dtype) for r in results),
        in_specs=[far] * k,
        out_specs=(far,) * k,
        scratch_shapes=[pltpu.VMEM(r.shape, r.dtype) for r in results]
        + [pltpu.SemaphoreType.DMA((k,)), pltpu.SemaphoreType.DMA((k,))],
        compiler_params=pltpu.CompilerParams(vmem_limit_bytes=60 * 1024 * 1024),
        name="hand_out",
    )(*results)


def per_device(n, g, *args):
    latent, feat, bias, route, tmask, wq, wk, wv, wo, gout = args
    lat_rows, width = latent.shape
    obs_rows = feat.shape[0]
    blocks, tiles = tmask.shape
    part = CAP * (obs_rows // blocks)
    key_rows = n * part
    chunks = width // LANES
    levels = n.bit_length() - 1
    rows = 4 * width // n
    two_step = (rows // g) % 16 == 0
    vm = pltpu.VMEM
    sem = pltpu.SemaphoreType.DMA
    weight = vm((width, width), BF16)
    scratch = [
        vm((lat_rows, width), BF16),
        vm((obs_rows, width), BF16),
        weight,
        weight,
        weight,
        weight,
        vm((lat_rows, width), BF16),
        sem((7,)),
        vm((width, lat_rows), BF16),
        vm((width, key_rows), BF16),
        vm((HEADS, key_rows, lat_rows), F32),
        vm((n, part, width + LANES), BF16),
        vm((n, part, width + LANES), BF16),
        vm((key_rows, obs_rows), BF16),
        vm((key_rows, lat_rows), F32),
        vm((lat_rows, width), BF16),
        vm((width, lat_rows), BF16),
        vm((lat_rows, width), BF16),
        vm((width, lat_rows), BF16),
        vm((key_rows, width), BF16),
        vm((key_rows, width), BF16),
        vm((width, key_rows), BF16),
        vm((width, key_rows), BF16),
        vm((width, lat_rows), BF16),
        vm((width, lat_rows), BF16),
        vm((key_rows, width), F32),
        vm((key_rows, width), F32),
        vm((lat_rows, width), BF16),
        vm((lat_rows, width), BF16),
        vm((n, part, width), BF16),
        vm((n, part, width), BF16),
        sem((n,)),
        sem((n,)),
        sem((n,)),
        sem((n,)),
        sem((chunks, levels)),
        sem((chunks, levels)),
        sem((chunks, g)),
        sem((chunks, g)),
        sem((chunks, g)),
        sem((chunks, g)),
    ]
    scratch += [vm((n // 2, 2, rows, LANES), BF16) for _ in range(chunks)]
    for c in range(chunks):
        for level in range(levels):
            scratch.append(vm((n >> (level + 1), rows, LANES), BF16))
        for level in range(levels):
            m = n >> (level + 1)
            if level == levels - 1:
                shape = (g, rows // g, LANES) if two_step else (rows, LANES)
            elif c % 2 == 0:
                shape = (m // 2, 2, rows, LANES)
            else:
                shape = (2, m // 2, rows, LANES)
            scratch.append(vm(shape, BF16))
    zr = rows // g if two_step else rows
    scratch.append(vm((chunks, g, zr, LANES), BF16))
    scratch.append(vm((chunks, zr, LANES), BF16))
    scratch.append(vm((chunks, g, zr, LANES), BF16))
    spec = pl.BlockSpec(memory_space=pltpu.VMEM)
    far = pl.BlockSpec(memory_space=pltpu.HBM)
    results = pl.pallas_call(
        functools.partial(kernel, n, g),
        out_shape=(
            jax.ShapeDtypeStruct((lat_rows, width), BF16),
            jax.ShapeDtypeStruct((lat_rows, width), BF16),
            jax.ShapeDtypeStruct((obs_rows, width), BF16),
            jax.ShapeDtypeStruct((rows, width), F32),
        ),
        in_specs=[far, far, spec, spec, spec, far, far, far, far, far],
        out_specs=(spec,) * 4,
        scratch_shapes=scratch,
        compiler_params=pltpu.CompilerParams(
            collective_id=0, has_side_effects=True, vmem_limit_bytes=60 * 1024 * 1024
        ),
        name="fused_layer",
    )(latent, feat, bias.reshape(1, obs_rows), route.T, tmask.T, wq, wk, wv, wo, gout)
    return hand_out(results)


def solution(mesh):
    n = mesh.shape["band"]
    g = mesh.shape["grp"]
    return jax.shard_map(
        functools.partial(per_device, n, g),
        mesh=mesh,
        in_specs=(
            P(("grp", "band"), None),
            P(("grp", "band"), None),
            P(("grp", "band")),
            P(("grp", "band"), None),
            P(("grp", "band"), None),
            P(),
            P(),
            P(),
            P(),
            P(("grp", "band"), None),
        ),
        out_specs=(
            P(("grp", "band"), None),
            P(("grp", "band"), None),
            P(("grp", "band"), None),
            P("band", None),
        ),
        check_vma=False,
    )
```
